128 devices in a mesh: segment: 2 (over x_hi), blk: 64 (over y, z, x_lo, core).
Axes of the slice: x: 4 (x_hi: 2, x_lo: 2; x = x_hi * 2 + x_lo), y: 4, z: 4, core: 2. Of those that a mesh axis runs over, the one named last changes fastest.
Arguments:
- slabs: bfloat16 [32, 2048, 2048], P(None, 'blk'), may hold values from -6 to 6
- orbitals: bfloat16 [2048, 1024], P('blk'), may hold values from -0.125 to 0.125
- channel_orbital: int32 [1024], replicated, may hold values from 0 to 1023
- channel_target: int32 [1024], replicated, may hold values from 0 to 15
- coupling: int32 [16, 16], replicated, may hold values from -16 to 16
Outputs:
- channel_block: bfloat16 [32, 1024, 1024], P(None, 'blk', 'segment')
The draws below stay inside these ranges and needn't reach their ends.
All inputs are finite; a program needn't handle non-finite values.
Results may differ from the reference program's by a relative error of at most 0.0056.
Values may be sent and summed in bfloat16 or wider, within the bound.
A program may use at most 64 MiB of HBM per device.

```python
import jax
import jax.numpy as jnp
from jax import lax

NB = 2048
NO = 1024
NCH = 1024
NT = 16
SLABS = 32


def plant(entries, key, least, largest):
    extent = entries.shape
    spot = [jax.random.randint(jax.random.fold_in(key, axis), (), 0, extent[axis]) for axis in range(len(extent))]
    entries = entries.at[tuple(spot)].set(least)
    longest = extent.index(max(extent))
    spot[longest] = (spot[longest] + 1) % extent[longest]
    return entries.at[tuple(spot)].set(largest)


def levels(own_key, shape, split, low, high):
    def one(axis_at, parts):
        steps = jax.random.uniform(jax.random.fold_in(jax.random.fold_in(own_key, 6), axis_at), (parts,), jnp.float32, low / len(split), high / len(split))
        return jnp.repeat(jnp.exp(steps), shape[axis_at] // parts).reshape((-1,) + (1,) * (len(shape) - axis_at - 1))

    loudness = one(*split[0])
    for cut in split[1:]:
        loudness = loudness * one(*cut)
    return loudness


def centred(key, shape, spread, bound, split=(), held_as=jnp.bfloat16):
    values = jax.random.normal(key, shape, jnp.float32) * spread
    if len(split) > 0:
        values = levels(key, shape, split, -0.22, 0.18) * values
    return jnp.clip(values, min=-bound, max=bound).astype(held_as)


def setup_inputs(seed: int = 0) -> dict:
    keys = jax.random.split(jax.random.key(seed), 6)
    slabs = centred(keys[0], (SLABS, NB, NB), 1.0, 6.0, ((1, 64),))
    orbitals = centred(keys[1], (NB, NO), NB ** -0.5, 0.125, ((0, 64),))
    channel_orbital = plant(jax.random.randint(keys[2], (NCH,), 0, NO), jax.random.fold_in(keys[2], 1), 0, NO - 1).astype(jnp.int32)
    channel_target = plant(jax.random.randint(keys[3], (NCH,), 0, NT), jax.random.fold_in(keys[3], 1), 0, NT - 1).astype(jnp.int32)
    coupling = plant(jax.random.randint(keys[4], (NT, NT), -16, 17), jax.random.fold_in(keys[4], 1), -16, 16).astype(jnp.int32)
    return {"slabs": slabs, "orbitals": orbitals, "channel_orbital": channel_orbital, "channel_target": channel_target, "coupling": coupling}


def reference(slabs, orbitals, channel_orbital, channel_target, coupling):
    angular = coupling[channel_target][:, channel_target].astype(jnp.float32) / 16.0

    def one_block(slab):
        half = jnp.dot(slab, orbitals, preferred_element_type=jnp.float32).astype(jnp.bfloat16)
        quarter = jnp.dot(orbitals.T, half, preferred_element_type=jnp.float32).astype(jnp.bfloat16)
        picked = quarter[channel_orbital][:, channel_orbital].astype(jnp.float32)
        return (angular * picked).astype(jnp.bfloat16)

    return lax.map(one_block, slabs)
```

```python
import functools

import jax
import jax.numpy as jnp
from jax import lax
from jax.experimental import pallas as pl
from jax.experimental.pallas import tpu as pltpu
from jax.sharding import PartitionSpec as P

SIDE = 4
ORDER = (2, 1, 3, 0)


def body(
    slabs_ref, orbitals_ref, channel_ref, target_ref, coupling_ref,
    out_ref, angular_ref,
    slab_v, c2, ct, half, panel, quarter,
    slab_sem, gather_send, gather_recv, sib_recv, swap_send, swap_recv, back_send, back_recv, own_sem,
):
    slabs, rows, depth = slab_v.shape
    blocks = panel.shape[0] // rows
    nch = ct.shape[0]
    cols = nch // 2
    part = cols // 2
    share = nch // blocks
    per_y = blocks // SIDE

    seg = lax.axis_index("segment")
    me = lax.axis_index("blk")
    core = me % 2
    pair = (me // 2) % 2
    z = (me // 4) % SIDE
    y = me // (4 * SIDE)
    sib = me + 1 - 2 * core
    across = me + 2 - 4 * pair
    a = y * (1 - core) + z * core
    b = z * (1 - core) + y * core

    def place(da, db):
        return ((a + da) % SIDE) * (4 - 3 * core) + ((b + db) % SIDE) * (1 + 3 * core)

    def at(da, db):
        return place(da, db) * 4 + pair * 2 + core

    partners = [sib, across, at(1, 0), at(3, 0), at(0, 1), at(0, 3)]
    load = pltpu.make_async_copy(slabs_ref, slab_v, slab_sem)
    load.start()
    barrier = pltpu.get_barrier_semaphore()
    for partner in partners:
        pl.semaphore_signal(barrier, inc=1, device_id={"blk": partner})

    my_rows = pl.multiple_of(me * rows, rows)
    mine = orbitals_ref[...]

    for piece in range(4):
        wide = nch // 4
        picks = channel_ref[:, piece * wide : (piece + 1) * wide]
        kinds = lax.broadcasted_iota(jnp.int32, (mine.shape[1], wide), 0)
        onehot = jnp.where(kinds == picks, 1.0, 0.0).astype(jnp.bfloat16)
        got = jnp.dot(mine, onehot, preferred_element_type=jnp.float32).astype(jnp.bfloat16)
        c2[piece // 2, pl.ds(my_rows, rows), (piece % 2) * wide : (piece % 2 + 1) * wide] = got

    pl.semaphore_wait(barrier, len(partners))

    started = []

    def push(view, device, index):
        copy = pltpu.make_async_remote_copy(
            src_ref=view, dst_ref=view,
            send_sem=gather_send.at[index], recv_sem=gather_recv.at[index],
            device_id={"blk": device},
        )
        copy.start()
        started.append(copy)

    def strip(start, count):
        return c2.at[core, pl.ds(pl.multiple_of(start, 32), count), :]

    def arrived(view, index):
        pltpu.make_async_copy(view, view, gather_recv.at[index]).wait()

    chip = 2 * rows
    square = 2 * chip
    forwarded = [22]

    def forward(start, count):
        view = strip(start, count)
        copy = pltpu.make_async_remote_copy(
            src_ref=view, dst_ref=view,
            send_sem=gather_send.at[forwarded[0]], recv_sem=sib_recv,
            device_id={"blk": sib},
        )
        forwarded[0] += 1
        copy.start()
        started.append(copy)

    both = c2.at[:, pl.ds(my_rows, rows), :]
    push(both, sib, 0)
    arrived(both, 0)
    push(strip(me // 2 * chip, chip), across, 1)
    arrived(strip(0, chip), 1)

    def start_of(da, db):
        return place(da, db) * square

    def along_b(j, da):
        push(strip(start_of(da, 0), square), at(0, 1), 6 + 4 * j)
        push(strip(start_of(da, 0), square), at(0, 3), 7 + 4 * j)

    push(strip(start_of(0, 0), square), at(1, 0), 2)
    push(strip(start_of(0, 0), square), at(3, 0), 3)
    along_b(0, 0)
    forward(across // 2 * chip, chip)
    arrived(strip(0, square), 2)
    push(strip(start_of(3, 0), chip), at(1, 0), 4)
    along_b(1, 3)
    forward(start_of(3, 0), square)
    arrived(strip(0, square), 3)
    push(strip(start_of(1, 0) + chip, chip), at(3, 0), 5)
    along_b(2, 1)
    forward(start_of(1, 0), square)

    def relay(j, da):
        arrived(strip(0, square), 6 + 4 * j)
        push(strip(start_of(da, 3), chip), at(0, 1), 8 + 4 * j)
        forward(start_of(da, 3), square)
        arrived(strip(0, square), 7 + 4 * j)
        push(strip(start_of(da, 1) + chip, chip), at(0, 3), 9 + 4 * j)
        forward(start_of(da, 1), square)

    def finish(j, da):
        arrived(strip(0, chip), 8 + 4 * j)
        arrived(strip(0, chip), 9 + 4 * j)
        forward(start_of(da, 2), square)

    relay(0, 0)
    arrived(strip(0, chip), 4)
    arrived(strip(0, chip), 5)
    along_b(3, 2)
    forward(start_of(2, 0), square)
    relay(1, 3)
    finish(0, 0)
    relay(2, 1)
    finish(1, 3)
    relay(3, 2)
    finish(2, 1)
    finish(3, 2)
    load.wait()
    others = blocks * rows - chip
    pltpu.make_async_copy(strip(0, others), strip(0, others), sib_recv).wait()

    def first(step, carry):
        group = (y + jnp.where(step == 0, ORDER[0], jnp.where(step == 1, ORDER[1], jnp.where(step == 2, ORDER[2], ORDER[3])))) % SIDE
        count = slabs // SIDE
        left = slab_v[pl.ds(group * count, count)].reshape(count * rows, depth)
        got = jnp.dot(left, c2[seg], preferred_element_type=jnp.float32).astype(jnp.bfloat16)
        got = got.reshape(count, rows, cols)
        for h in range(2):
            half[pl.ds(group * count, count), h] = got[:, :, h * part : (h + 1) * part]

        def send(i, carry):
            peer = group * per_y + (me + i) % per_y

            @pl.when(peer != me)
            def _():
                pltpu.make_async_remote_copy(
                    src_ref=half.at[peer // 2, peer % 2],
                    dst_ref=panel.at[pl.ds(my_rows, rows), :],
                    send_sem=swap_send, recv_sem=swap_recv,
                    device_id={"blk": peer},
                ).start()

            return carry

        return lax.fori_loop(0, per_y, send, carry)

    lax.fori_loop(0, SIDE, first, 0)
    panel[pl.ds(my_rows, rows), :] = half[me // 2, core]

    def turn(i, carry):
        start = pl.multiple_of(i * 256, 256)
        for k in range(2):
            ct[k * cols : (k + 1) * cols, pl.ds(start, 256)] = c2[k, pl.ds(start, 256), :].T
        return carry

    lax.fori_loop(0, depth // 256, turn, 0)

    nt = coupling_ref.shape[0]
    kinds = lax.broadcasted_iota(jnp.int32, (nt, nch), 0)
    hot = jnp.where(kinds == target_ref[...], 1.0, 0.0).astype(jnp.bfloat16)
    channel = lax.broadcasted_iota(jnp.int32, (share, nch), 1)
    line = lax.broadcasted_iota(jnp.int32, (share, nch), 0)
    pick = jnp.where(channel == line + me * share, 1.0, 0.0).astype(jnp.bfloat16)
    dims = (((1,), (1,)), ((), ()))
    hot_rows = lax.dot_general(pick, hot, dims, preferred_element_type=jnp.float32).astype(jnp.bfloat16)
    table = coupling_ref[...].astype(jnp.float32).astype(jnp.bfloat16)
    mixed = jnp.dot(hot_rows, table, preferred_element_type=jnp.float32).astype(jnp.bfloat16)
    angular = jnp.dot(mixed, hot, preferred_element_type=jnp.float32) * (1.0 / 16.0)
    angular_ref[...] = jnp.where(seg == 0, angular[:, :cols], angular[:, cols:])

    rest = (blocks - 1) * rows
    pltpu.make_async_copy(panel.at[pl.ds(0, rest), :], panel.at[pl.ds(0, rest), :], swap_recv).wait()

    my_cols = pl.multiple_of(core * part, part)

    def second(step, carry):
        group = (y + jnp.where(step == 0, ORDER[0], jnp.where(step == 1, ORDER[1], jnp.where(step == 2, ORDER[2], ORDER[3])))) % SIDE
        count = nch // SIDE
        left = ct[pl.ds(pl.multiple_of(group * count, count), count), :]
        got = jnp.dot(left, panel[...], preferred_element_type=jnp.float32).astype(jnp.bfloat16)
        quarter[pl.ds(group * per_y, per_y)] = got.reshape(per_y, share, part)

        def send(i, carry):
            peer = group * per_y + (me + i) % per_y

            @pl.when(peer != me)
            def _():
                pltpu.make_async_remote_copy(
                    src_ref=quarter.at[peer],
                    dst_ref=out_ref.at[me // 2, :, pl.ds(my_cols, part)],
                    send_sem=back_send, recv_sem=back_recv,
                    device_id={"blk": peer},
                ).start()

            return carry

        return lax.fori_loop(0, per_y, send, carry)

    lax.fori_loop(0, SIDE, second, 0)
    own = pltpu.make_async_copy(quarter.at[me], out_ref.at[me // 2, :, pl.ds(my_cols, part)], own_sem)
    own.start()
    own.wait()
    for copy in started:
        copy.wait_send()
    pltpu.make_async_copy(panel.at[pl.ds(0, rest), :], panel.at[pl.ds(0, rest), :], swap_send).wait()
    last = quarter.at[pl.ds(0, blocks - 1)]
    pltpu.make_async_copy(last, last, back_send).wait()
    pltpu.make_async_copy(last, last, back_recv).wait()


def on_device(slabs, orbitals, channel_orbital, channel_target, coupling):
    blocks = lax.axis_size("blk")
    count, rows, depth = slabs.shape
    nch = channel_orbital.shape[0]
    cols = nch // 2
    part = cols // 2
    share = nch // blocks
    vmem = pl.BlockSpec(memory_space=pltpu.VMEM)
    anywhere = pl.BlockSpec(memory_space=pl.ANY)
    dma = pltpu.SemaphoreType.DMA
    picked, angular = pl.pallas_call(
        body,
        out_shape=(
            jax.ShapeDtypeStruct((count, share, cols), jnp.bfloat16),
            jax.ShapeDtypeStruct((share, cols), jnp.float32),
        ),
        in_specs=[anywhere, vmem, vmem, vmem, vmem],
        out_specs=(anywhere, vmem),
        scratch_shapes=[
            pltpu.VMEM((count, rows, depth), jnp.bfloat16),
            pltpu.VMEM((2, depth, cols), jnp.bfloat16),
            pltpu.VMEM((nch, depth), jnp.bfloat16),
            pltpu.VMEM((count, 2, rows, part), jnp.bfloat16),
            pltpu.VMEM((depth, part), jnp.bfloat16),
            pltpu.VMEM((blocks, share, part), jnp.bfloat16),
            dma, dma((38,)), dma((22,)), dma, dma, dma, dma, dma, dma,
        ],
        compiler_params=pltpu.CompilerParams(
            collective_id=0, has_side_effects=True, vmem_limit_bytes=48 * 1024 * 1024
        ),
        name="transform",
    )(slabs, orbitals, channel_orbital.reshape(1, nch), channel_target.reshape(1, nch), coupling)
    return (angular[None] * picked.astype(jnp.float32)).astype(jnp.bfloat16)


def solution(mesh):
    return jax.shard_map(
        on_device,
        mesh=mesh,
        in_specs=(P(None, "blk", None), P("blk", None), P(), P(), P()),
        out_specs=P(None, "blk", "segment"),
        check_vma=False,
    )
```

```python
import jax
import jax.numpy as jnp
from jax import lax
from jax.experimental import pallas as pl
from jax.experimental.pallas import tpu as pltpu
from jax.sharding import PartitionSpec as P

SIDE = 4
CHUNKS = 2
RINGED = (1,)
CROSSED = (0,)
LATE = 0
DIMS = (((1,), (1,)), ((), ()))


def shifted(step):
    return jnp.where(step == 0, 2, jnp.where(step == 1, 1, jnp.where(step == 2, 3, 0)))


def body(
    slabs_ref, orbitals_ref, channel_ref, target_ref, coupling_ref,
    out_ref, angular_ref,
    slab_v, orb_v, channel_v, target_v, coupling_v, c, ct, half, panel, quarter,
    load_sem, near_send, near_recv, far_send, far_recv, sib_send, sib_recv,
    cross_send, cross_recv, over_send, over_recv,
    swap_send, swap_recv, back_send, back_recv, own_sem,
):
    slabs, rows, depth = slab_v.shape
    blocks = depth // rows
    nch = ct.shape[0]
    cols = nch // 2
    part = cols // 2
    w = part // CHUNKS
    share = nch // blocks
    per_y = blocks // SIDE

    seg = lax.axis_index("segment")
    me = lax.axis_index("blk")
    core = me % 2
    pair = (me // 2) % 2
    z = (me // 4) % SIDE
    y = me // (4 * SIDE)
    sib = me + 1 - 2 * core
    cross = {"blk": me + 2 - 4 * pair, "segment": 1 - seg}
    a = y * (1 - core) + z * core
    b = z * (1 - core) + y * core

    def at(da, dx, db):
        spot = ((a + da) % SIDE) * (4 - 3 * core) + ((b + db) % SIDE) * (1 + 3 * core)
        return spot * 4 + ((pair + dx) % 2) * 2 + core

    loads = [
        pltpu.make_async_copy(src, dst, load_sem.at[i])
        for i, (src, dst) in enumerate([
            (channel_ref, channel_v), (orbitals_ref, orb_v), (target_ref, target_v),
            (coupling_ref, coupling_v), (slabs_ref, slab_v),
        ])
    ]
    for load in loads:
        load.start()

    barrier = pltpu.get_barrier_semaphore()
    near = [(da, dx) for dx in range(2) for da in (0, 2, 1, 3) if (da, dx) != (0, 0)]
    for da, dx in near:
        pl.semaphore_signal(barrier, inc=1, device_id={"blk": at(da, dx, 0)})
    for db in range(1, SIDE):
        pl.semaphore_signal(barrier, inc=1, device_id={"blk": at(0, 0, db)})
    pl.semaphore_signal(barrier, inc=1, device_id={"blk": sib})
    pl.semaphore_signal(barrier, inc=1, device_id=cross)

    def block(which, q):
        return c.at[which, q, y, z, pair, core]

    def group(k, which, q, db):
        at_b = (b + db) % SIDE
        return c.at[which, q, :, at_b, :, 0] if k == 0 else c.at[which, q, at_b, :, :, 1]

    def each_core(do):
        for k in range(2):
            @pl.when(core == k)
            def _():
                do(k)

    def send(view, send_sem, recv_sem, device):
        device = device if isinstance(device, dict) else {"blk": device}
        pltpu.make_async_remote_copy(
            src_ref=view, dst_ref=view, send_sem=send_sem, recv_sem=recv_sem, device_id=device
        ).start()

    def arrived(sem, count):
        view = half.at[0, pl.ds(0, count)]
        pltpu.make_async_copy(view, view, sem).wait()

    strands = [(seg, q, q) for q in range(CHUNKS)] + [(1 - seg, q, CHUNKS + i) for i, q in enumerate(RINGED)]

    def make_block(t):
        which, q, _ = strands[t]
        picks = []
        for h in range(2):
            start = pl.multiple_of(which * cols + (h * part + q * w), w)
            picks.append(channel_v[:, pl.ds(start, w)])
        picks = jnp.concatenate(picks, axis=1)
        kinds = lax.broadcasted_iota(jnp.int32, (mine.shape[1], 2 * w), 0)
        onehot = jnp.where(kinds == picks, 1.0, 0.0).astype(jnp.bfloat16)
        got = jnp.dot(mine, onehot, preferred_element_type=jnp.float32).astype(jnp.bfloat16)
        c[which, q, y, z, pair, core] = got

    def near_out(t):
        which, q, _ = strands[t]
        for da, dx in near:
            send(block(which, q), near_send.at[t], near_recv.at[t], at(da, dx, 0))

    def pass_on(t, db):
        which, q, _ = strands[t]

        def do(k):
            view = group(k, which, q, -db)
            if db == 0:
                for far in (2, 1, 3):
                    send(view, far_send.at[t], far_recv.at[t, far - 1], at(0, 0, far))
            send(view, sib_send.at[t], sib_recv.at[t], sib)
            if t < CHUNKS and q not in RINGED:
                send(view, cross_send.at[q], cross_recv.at[q, db], cross)

        each_core(do)

    def near_in(t):
        arrived(near_recv.at[t], 7)
        pass_on(t, 0)

    def far_in(t):
        for db in (1, 3, 2):
            arrived(far_recv.at[t, db - 1], 8)
            pass_on(t, db)

    loads[0].wait()
    loads[1].wait()
    mine = orb_v[...]
    for t in range(len(strands)):
        make_block(t)
        if t == 0:
            pl.semaphore_wait(barrier, len(near) + SIDE + 1)
        if t < CHUNKS or not LATE:
            near_out(t)

    for t in range(len(strands) if not LATE else CHUNKS):
        near_in(t)

    def first(q):
        def one(step, carry):
            group = (y + shifted(step)) % SIDE
            count = slabs // SIDE
            left = slab_v[pl.ds(group * count, count)].reshape(count * rows, depth)
            got = jnp.dot(left, c[seg, q].reshape(depth, 2 * w), preferred_element_type=jnp.float32).astype(jnp.bfloat16)
            got = got.reshape(count, rows, 2 * w)
            for h in range(2):
                half[q, pl.ds(group * count, count), h] = got[:, :, h * w : (h + 1) * w]

            def go(i, carry):
                peer = group * per_y + (me + i) % per_y

                @pl.when(peer != me)
                def _():
                    pltpu.make_async_remote_copy(
                        src_ref=half.at[q, peer // 2, peer % 2],
                        dst_ref=panel.at[q, pl.ds(pl.multiple_of(me * rows, rows), rows), :],
                        send_sem=swap_send.at[q], recv_sem=swap_recv.at[q],
                        device_id={"blk": peer},
                    ).start()

                return carry

            return lax.fori_loop(0, per_y, go, carry)

        lax.fori_loop(0, SIDE, one, 0)
        panel[q, pl.ds(pl.multiple_of(me * rows, rows), rows), :] = half[q, me // 2, core]

    for q in range(CHUNKS):
        far_in(q)
        arrived(sib_recv.at[q], blocks // 2)
        if q == 0:
            loads[4].wait()
        first(q)
        if LATE and q == LATE - 1:
            for t in range(CHUNKS, len(strands)):
                near_out(t)

    if LATE:
        for t in range(CHUNKS, len(strands)):
            near_in(t)
    for q in CROSSED:
        for db in (0, 1, 3, 2):
            arrived(cross_recv.at[q, db], 2 * SIDE)
            each_core(lambda k: send(group(k, 1 - seg, q, -db), over_send.at[q], over_recv.at[q], sib))
    for t in range(CHUNKS, len(strands)):
        far_in(t)

    def turn(which):
        for q in range(CHUNKS):
            def one(i, carry):
                start = pl.multiple_of(i * 256, 256)
                for h in range(2):
                    top = pl.multiple_of(which * cols + (h * part + q * w), w)
                    piece = c[which, q, i // 2, pl.ds(i % 2 * 2, 2), :, :, :, h * w : (h + 1) * w]
                    ct[pl.ds(top, w), pl.ds(start, 256)] = piece.reshape(256, w).T
                return carry

            lax.fori_loop(0, depth // 256, one, 0)

    turn(seg)

    loads[2].wait()
    loads[3].wait()
    nt = coupling_v.shape[0]
    kinds = lax.broadcasted_iota(jnp.int32, (nt, nch), 0)
    hot = jnp.where(kinds == target_v[...], 1.0, 0.0).astype(jnp.bfloat16)
    channel = lax.broadcasted_iota(jnp.int32, (share, nch), 1)
    line = lax.broadcasted_iota(jnp.int32, (share, nch), 0)
    pick = jnp.where(channel == line + me * share, 1.0, 0.0).astype(jnp.bfloat16)
    hot_rows = lax.dot_general(pick, hot, DIMS, preferred_element_type=jnp.float32).astype(jnp.bfloat16)
    table = coupling_v[...].astype(jnp.float32).astype(jnp.bfloat16)
    mixed = jnp.dot(hot_rows, table, preferred_element_type=jnp.float32).astype(jnp.bfloat16)
    angular = jnp.dot(mixed, hot, preferred_element_type=jnp.float32) * (1.0 / 16.0)
    angular_ref[...] = jnp.where(seg == 0, angular[:, :cols], angular[:, cols:])

    for q in CROSSED:
        arrived(over_recv.at[q], blocks // 2)
    for t in range(CHUNKS, len(strands)):
        arrived(sib_recv.at[t], blocks // 2)
    turn(1 - seg)

    def out_at(q):
        return out_ref.at[me // 2, :, pl.ds(pl.multiple_of(core * part + q * w, w), w)]

    def second(q):
        def one(step, carry):
            group = (y + shifted(step)) % SIDE
            count = nch // SIDE
            left = ct[pl.ds(pl.multiple_of(group * count, count), count), :]
            got = jnp.dot(left, panel[q], preferred_element_type=jnp.float32).astype(jnp.bfloat16)
            quarter[q, pl.ds(group * per_y, per_y)] = got.reshape(per_y, share, w)

            def go(i, carry):
                peer = group * per_y + (me + i) % per_y

                @pl.when(peer != me)
                def _():
                    pltpu.make_async_remote_copy(
                        src_ref=quarter.at[q, peer], dst_ref=out_at(q),
                        send_sem=back_send.at[q], recv_sem=back_recv.at[q],
                        device_id={"blk": peer},
                    ).start()

                return carry

            return lax.fori_loop(0, per_y, go, carry)

        lax.fori_loop(0, SIDE, one, 0)
        pltpu.make_async_copy(quarter.at[q, me], out_at(q), own_sem.at[q]).start()

    for q in range(CHUNKS):
        some = panel.at[q, pl.ds(0, (blocks - 1) * rows), :]
        pltpu.make_async_copy(some, some, swap_recv.at[q]).wait()
        second(q)

    for q in range(CHUNKS):
        some = panel.at[q, pl.ds(0, (blocks - 1) * rows), :]
        last = quarter.at[q, pl.ds(0, blocks - 1)]
        if q == 0:
            for t in range(len(strands)):
                arrived(near_send.at[t], 7)
                arrived(far_send.at[t], 24)
                arrived(sib_send.at[t], blocks // 2)
            for other in CROSSED:
                arrived(cross_send.at[other], blocks // 2)
                arrived(over_send.at[other], blocks // 2)
        pltpu.make_async_copy(some, some, swap_send.at[q]).wait()
        pltpu.make_async_copy(last, last, back_send.at[q]).wait()
        pltpu.make_async_copy(last, last, back_recv.at[q]).wait()
        pltpu.make_async_copy(quarter.at[q, me], out_at(q), own_sem.at[q]).wait()


def on_device(slabs, orbitals, channel_orbital, channel_target, coupling):
    blocks = lax.axis_size("blk")
    count, rows, depth = slabs.shape
    nch = channel_orbital.shape[0]
    cols = nch // 2
    w = cols // 2 // CHUNKS
    share = nch // blocks
    hbm = pl.BlockSpec(memory_space=pltpu.HBM)
    anywhere = pl.BlockSpec(memory_space=pl.ANY)
    dma = pltpu.SemaphoreType.DMA
    vmem = pltpu.VMEM
    picked, angular = pl.pallas_call(
        body,
        out_shape=(
            jax.ShapeDtypeStruct((count, share, cols), jnp.bfloat16),
            jax.ShapeDtypeStruct((share, cols), jnp.float32),
        ),
        in_specs=[hbm] * 5,
        out_specs=(anywhere, pl.BlockSpec(memory_space=vmem)),
        scratch_shapes=[
            vmem((count, rows, depth), jnp.bfloat16),
            vmem(orbitals.shape, jnp.bfloat16),
            vmem((1, nch), jnp.int32),
            vmem((1, nch), jnp.int32),
            vmem(coupling.shape, jnp.int32),
            vmem((2, CHUNKS, SIDE, SIDE, 2, 2, rows, 2 * w), jnp.bfloat16),
            vmem((nch, depth), jnp.bfloat16),
            vmem((CHUNKS, count, 2, rows, w), jnp.bfloat16),
            vmem((CHUNKS, depth, w), jnp.bfloat16),
            vmem((CHUNKS, blocks, share, w), jnp.bfloat16),
            dma((5,)),
            dma((4,)), dma((4,)), dma((4,)), dma((4, 3)), dma((4,)), dma((4,)),
            dma((CHUNKS,)), dma((CHUNKS, 4)), dma((CHUNKS,)), dma((CHUNKS,)),
            dma((CHUNKS,)), dma((CHUNKS,)), dma((CHUNKS,)), dma((CHUNKS,)), dma((CHUNKS,)),
        ],
        compiler_params=pltpu.CompilerParams(
            collective_id=0, has_side_effects=True, vmem_limit_bytes=48 * 1024 * 1024
        ),
        name="transform",
    )(*[
        pltpu.with_memory_space_constraint(v, pltpu.HBM)
        for v in (slabs, orbitals, channel_orbital.reshape(1, nch), channel_target.reshape(1, nch), coupling)
    ])
    return (angular[None] * picked.astype(jnp.float32)).astype(jnp.bfloat16)


def solution(mesh):
    return jax.shard_map(
        on_device,
        mesh=mesh,
        in_specs=(P(None, "blk", None), P("blk", None), P(), P(), P()),
        out_specs=P(None, "blk", "segment"),
        check_vma=False,
    )
```

```python
import jax
import jax.numpy as jnp
from jax import lax
from jax.experimental import pallas as pl
from jax.experimental.pallas import tpu as pltpu
from jax.sharding import PartitionSpec as P

SIDE = 4
PIECES = 2
RINGED = ((), (1, 3))
EARLY = (1,)
FIRSTS = ((0, 1), (0, 3), (1, 1), (1, 3), (0, 2), (1, 2))
LASTS = ()
LATE = 0
NEAR = (0, 3, 1, 2, 5, 6, 4, 7)
DIMS = (((1,), (1,)), ((), ()))


def shifted(step):
    return jnp.where(step == 0, 2, jnp.where(step == 1, 1, jnp.where(step == 2, 3, 0)))


def body(
    slabs_ref, orbitals_ref, channel_ref, target_ref, coupling_ref,
    out_ref, angular_ref,
    slab_v, orb_v, channel_v, target_v, coupling_v, own, c, ct, half, panel, quarter,
    load_sem, near_send, near_recv, far_send, far_recv, sib_send, sib_recv,
    cross_send, cross_recv, other_send, other_recv, over_send, over_recv,
    swap_send, swap_recv, back_send, back_recv, own_sem,
):
    slabs, rows, depth = slab_v.shape
    blocks = depth // rows
    nch = ct.shape[0]
    cols = nch // 2
    part = cols // 2
    w = part // PIECES
    share = nch // blocks
    per_y = blocks // SIDE

    seg = lax.axis_index("segment")
    me = lax.axis_index("blk")
    core = me % 2
    pair = (me // 2) % 2
    z = (me // 4) % SIDE
    y = me // (4 * SIDE)
    sib = me + 1 - 2 * core
    across = me + 2 - 4 * pair
    cross = {"blk": across, "segment": 1 - seg}
    a = y * (1 - core) + z * core
    b = z * (1 - core) + y * core

    def at(da, dx, db, flip=0):
        spot = ((a + da) % SIDE) * (4 - 3 * core) + ((b + db) % SIDE) * (1 + 3 * core)
        return spot * 4 + ((pair + dx) % 2) * 2 + (core + flip) % 2

    loads = [
        pltpu.make_async_copy(src, dst, load_sem.at[i])
        for i, (src, dst) in enumerate([
            (channel_ref, channel_v), (orbitals_ref, orb_v), (target_ref, target_v),
            (coupling_ref, coupling_v), (slabs_ref, slab_v),
        ])
    ]
    for load in loads:
        load.start()

    near = [(0, 0), (1, 0), (3, 0), (0, 1), (2, 0), (1, 1), (3, 1), (2, 1)]
    partners = [at(da, dx, 0) for da, dx in near[1:]] + [at(da, dx, 0, 1) for da, dx in near]
    partners += [at(0, dx, db, 1) for db, dx in near if db] + [at(0, 0, db) for db in range(1, SIDE)]
    barrier = pltpu.get_barrier_semaphore()
    for partner in partners:
        pl.semaphore_signal(barrier, inc=1, device_id={"blk": partner})
    pl.semaphore_signal(barrier, inc=1, device_id=cross)

    def group(k, which, j, db):
        at_b = (b + db) % SIDE
        return c.at[which, 0, j, :, at_b] if k == 0 else c.at[which, 1, j, at_b]

    def chip(which, j, da, dx):
        pa = (a + da) % SIDE
        return c.at[which, core, j, pa * (1 - core) + b * core, b * (1 - core) + pa * core, (pair + dx) % 2]

    def each_core(do):
        for k in range(2):
            @pl.when(core == k)
            def _():
                do(k)

    def send(view, send_sem, recv_sem, device, dst=None):
        device = device if isinstance(device, dict) else {"blk": device}
        pltpu.make_async_remote_copy(
            src_ref=view, dst_ref=view if dst is None else dst,
            send_sem=send_sem, recv_sem=recv_sem, device_id=device,
        ).start()

    def arrived(sem, count):
        view = panel.at[0, pl.ds(0, count * rows), :]
        pltpu.make_async_copy(view, view, sem).wait()

    def make(j):
        picks = [
            channel_v[:, pl.ds(pl.multiple_of(seg * cols + (q * part + j * w), w), w)] for q in range(2)
        ]
        picks = jnp.concatenate(picks, axis=1)
        kinds = lax.broadcasted_iota(jnp.int32, (mine.shape[1], 2 * w), 0)
        onehot = jnp.where(kinds == picks, 1.0, 0.0).astype(jnp.bfloat16)
        got = jnp.dot(mine, onehot, preferred_element_type=jnp.float32).astype(jnp.bfloat16)
        for q in range(2):
            own[j, q] = got[:, q * w : (q + 1) * w]
        c[seg, core, j, y, z, pair, core] = own[j, core]

    def near_out(j):
        for i in NEAR:
            da, dx = near[i]
            recv = near_recv.at[j, i]
            if i:
                send(own.at[j, core], near_send.at[j], recv, at(da, dx, 0), c.at[seg, core, j, y, z, pair, core])
            send(
                own.at[j, 1 - core], near_send.at[j], recv, at(0, dx, da, 1),
                c.at[seg, 1 - core, j, y, z, pair, core],
            )

    def near_in(j):
        for i in NEAR:
            da, dx = near[i]
            arrived(near_recv.at[j, i], 2 if i else 1)
            view = chip(seg, j, -da, dx)
            for far in (2, 1, 3):
                send(view, far_send.at[j], far_recv.at[j, far - 1], at(0, 0, far))
            send(view, cross_send.at[j], cross_recv.at[j, 0], cross)
        each_core(lambda k: send(group(k, seg, j, 0), sib_send.at[j], sib_recv.at[j], sib))

    def far_in(j):
        for db in (1, 3, 2):
            arrived(far_recv.at[j, db - 1], 16)

            def do(k):
                view = group(k, seg, j, -db)
                send(view, sib_send.at[j], sib_recv.at[j], sib)
                if db not in RINGED[j]:
                    send(view, cross_send.at[j], cross_recv.at[j, db], cross)

            each_core(do)

    def other_in(j, db):
        arrived(other_recv.at[j, db - 1] if db in RINGED[j] else cross_recv.at[j, db], 16)

        def do(k):
            view = group(k, 1 - seg, j, -db)
            if db == 0:
                for far in RINGED[j]:
                    send(view, other_send.at[j], other_recv.at[j, far - 1], at(0, 0, far))
            send(view, over_send.at[j], over_recv.at[j], sib)

        each_core(do)

    def first(q, j):
        my_rows = pl.ds(pl.multiple_of(me * rows, rows), rows)

        def one(step, carry):
            at_y = (y + shifted(step)) % SIDE
            count = slabs // SIDE
            left = slab_v[pl.ds(at_y * count, count)].reshape(count * rows, depth)
            got = jnp.dot(left, c[seg, q, j].reshape(depth, w), preferred_element_type=jnp.float32)
            half[q, j, pl.ds(at_y * count, count)] = got.astype(jnp.bfloat16).reshape(count, rows, w)

            def go(i, carry):
                slab = at_y * count + (me // 2 + i) % count
                peer = slab * 2 + q

                @pl.when(peer != me)
                def _():
                    send(half.at[q, j, slab], swap_send.at[j], swap_recv.at[j], peer, panel.at[j, my_rows, :])

                return carry

            return lax.fori_loop(0, count, go, carry)

        lax.fori_loop(0, SIDE, one, 0)

    def turn(which):
        def one(i, carry):
            start = pl.multiple_of(i * 256, 256)
            for q in range(2):
                for j in range(PIECES):
                    top = pl.multiple_of(which * cols + (q * part + j * w), w)
                    piece = c[which, q, j, i // 2, pl.ds(i % 2 * 2, 2)].reshape(256, w)
                    ct[pl.ds(top, w), pl.ds(start, 256)] = piece.T
            return carry

        lax.fori_loop(0, depth // 256, one, 0)

    loads[0].wait()
    loads[1].wait()
    mine = orb_v[...]
    make(0)
    pl.semaphore_wait(barrier, len(partners) + 1)
    near_out(0)
    make(1)
    near_out(1)
    near_in(0)
    near_in(1)
    far_in(0)
    loads[4].wait()
    first(core, 0)
    for j in EARLY:
        other_in(j, 0)
    arrived(sib_recv.at[0], blocks)
    first(1 - core, 0)
    far_in(1)
    first(core, 1)
    arrived(sib_recv.at[1], blocks)
    first(1 - core, 1)
    for j in range(PIECES):
        panel[j, pl.ds(pl.multiple_of(me * rows, rows), rows), :] = half[core, j, me // 2]
    turn(seg)

    loads[2].wait()
    loads[3].wait()
    nt = coupling_v.shape[0]
    kinds = lax.broadcasted_iota(jnp.int32, (nt, nch), 0)
    hot = jnp.where(kinds == target_v[...], 1.0, 0.0).astype(jnp.bfloat16)
    channel = lax.broadcasted_iota(jnp.int32, (share, nch), 1)
    line = lax.broadcasted_iota(jnp.int32, (share, nch), 0)
    pick = jnp.where(channel == line + me * share, 1.0, 0.0).astype(jnp.bfloat16)
    hot_rows = lax.dot_general(pick, hot, DIMS, preferred_element_type=jnp.float32).astype(jnp.bfloat16)
    table = coupling_v[...].astype(jnp.float32).astype(jnp.bfloat16)
    mixed = jnp.dot(hot_rows, table, preferred_element_type=jnp.float32).astype(jnp.bfloat16)
    angular = jnp.dot(mixed, hot, preferred_element_type=jnp.float32) * (1.0 / 16.0)
    angular_ref[...] = jnp.where(seg == 0, angular[:, :cols], angular[:, cols:])

    for j in range(PIECES):
        if j not in EARLY:
            other_in(j, 0)
    for j, db in FIRSTS:
        other_in(j, db)

    def out_at(j):
        return out_ref.at[me // 2, :, pl.ds(pl.multiple_of(core * part + j * w, w), w)]

    def second(j, which):
        def one(step, carry):
            at_y = 2 * which + (y + 1 + step) % 2
            count = nch // SIDE
            left = ct[pl.ds(pl.multiple_of(at_y * count, count), count), :]
            got = jnp.dot(left, panel[j], preferred_element_type=jnp.float32).astype(jnp.bfloat16)
            quarter[j, pl.ds(at_y * per_y, per_y)] = got.reshape(per_y, share, w)

            def go(i, carry):
                peer = at_y * per_y + (me + i) % per_y

                @pl.when(peer != me)
                def _():
                    send(quarter.at[j, peer], back_send.at[j], back_recv.at[j], peer, out_at(j))

                return carry

            return lax.fori_loop(0, per_y, go, carry)

        lax.fori_loop(0, SIDE // 2, one, 0)

    arrived(swap_recv.at[0], blocks - 1)
    second(0, seg)
    if LATE:
        pass
        arrived(swap_recv.at[1], blocks - 1)
        second(1, seg)
    for j, db in LASTS:
        other_in(j, db)
    for j in range(PIECES):
        arrived(over_recv.at[j], blocks)
    turn(1 - seg)
    second(0, 1 - seg)
    if not LATE:
        pass
        arrived(swap_recv.at[1], blocks - 1)
        second(1, seg)
    second(1, 1 - seg)
    kept = [pltpu.make_async_copy(quarter.at[j, me], out_at(j), own_sem.at[j]) for j in range(PIECES)]
    for copy in kept:
        copy.start()
    for copy in kept:
        copy.wait()

    for j in range(PIECES):
        last = quarter.at[j, pl.ds(0, blocks - 1)]
        arrived(near_send.at[j], 15)
        arrived(far_send.at[j], 48)
        arrived(sib_send.at[j], blocks)
        arrived(cross_send.at[j], 16 * (4 - len(RINGED[j])))
        if RINGED[j]:
            arrived(other_send.at[j], 16 * len(RINGED[j]))
        arrived(over_send.at[j], blocks)
        arrived(swap_send.at[j], blocks - 1)
        pltpu.make_async_copy(last, last, back_send.at[j]).wait()
        pltpu.make_async_copy(last, last, back_recv.at[j]).wait()


def on_device(slabs, orbitals, channel_orbital, channel_target, coupling):
    blocks = lax.axis_size("blk")
    count, rows, depth = slabs.shape
    nch = channel_orbital.shape[0]
    cols = nch // 2
    part = cols // 2
    w = part // PIECES
    share = nch // blocks
    hbm = pl.BlockSpec(memory_space=pltpu.HBM)
    dma = pltpu.SemaphoreType.DMA
    each = dma((PIECES,))
    vmem = pltpu.VMEM
    picked, angular = pl.pallas_call(
        body,
        out_shape=(
            jax.ShapeDtypeStruct((count, share, cols), jnp.bfloat16),
            jax.ShapeDtypeStruct((share, cols), jnp.float32),
        ),
        in_specs=[hbm] * 5,
        out_specs=(pl.BlockSpec(memory_space=pl.ANY), pl.BlockSpec(memory_space=vmem)),
        scratch_shapes=[
            vmem((count, rows, depth), jnp.bfloat16),
            vmem(orbitals.shape, jnp.bfloat16),
            vmem((1, nch), jnp.int32),
            vmem((1, nch), jnp.int32),
            vmem(coupling.shape, jnp.int32),
            vmem((PIECES, 2, rows, w), jnp.bfloat16),
            vmem((2, 2, PIECES, SIDE, SIDE, 2, 2, rows, w), jnp.bfloat16),
            vmem((nch, depth), jnp.bfloat16),
            vmem((2, PIECES, count, rows, w), jnp.bfloat16),
            vmem((PIECES, depth, w), jnp.bfloat16),
            vmem((PIECES, blocks, share, w), jnp.bfloat16),
            dma((5,)), each, dma((PIECES, 8)), each, dma((PIECES, 3)), each, each,
            each, dma((PIECES, 4)), each, dma((PIECES, 3)), each, each,
            each, each, each, each, each,
        ],
        compiler_params=pltpu.CompilerParams(
            collective_id=0, has_side_effects=True, vmem_limit_bytes=48 * 1024 * 1024
        ),
        name="transform",
    )(*[
        pltpu.with_memory_space_constraint(v, pltpu.HBM)
        for v in (slabs, orbitals, channel_orbital.reshape(1, nch), channel_target.reshape(1, nch), coupling)
    ])
    return (angular[None] * picked.astype(jnp.float32)).astype(jnp.bfloat16)


def solution(mesh):
    return jax.shard_map(
        on_device,
        mesh=mesh,
        in_specs=(P(None, "blk", None), P("blk", None), P(), P(), P()),
        out_specs=P(None, "blk", "segment"),
        check_vma=False,
    )
```

```python
import jax
import jax.numpy as jnp
from jax import lax
from jax.experimental import pallas as pl
from jax.experimental.pallas import tpu as pltpu
from jax.sharding import PartitionSpec as P

SIDE = 4
PIECES = 2
RINGED = ((), (1, 3))
EARLY = (1,)
FIRSTS = ((0, 1), (0, 3), (1, 1), (1, 3), (0, 2), (1, 2))
LASTS = ()
LATE = 0
LAG = 1
NEAR = (0, 3, 1, 2, 5, 6, 4, 7)
DIMS = (((1,), (1,)), ((), ()))


def body(
    slabs_ref, orbitals_ref, channel_ref, target_ref, coupling_ref,
    out_ref, angular_ref,
    slab_v, orb_v, channel_v, target_v, coupling_v, own, c, ct, half, panel, quarter,
    load_sem, near_send, near_recv, far_send, far_recv, sib_send, sib_recv,
    cross_send, cross_recv, other_send, other_recv, over_send, over_recv,
    swap_send, swap_recv, back_send, back_recv, own_sem,
):
    slabs, rows, depth = slab_v.shape
    blocks = depth // rows
    nch = ct.shape[0]
    cols = nch // 2
    part = cols // 2
    w = part // PIECES
    share = nch // blocks
    per_y = blocks // SIDE

    seg = lax.axis_index("segment")
    me = lax.axis_index("blk")
    core = me % 2
    pair = (me // 2) % 2
    z = (me // 4) % SIDE
    y = me // (4 * SIDE)
    sib = me + 1 - 2 * core
    across = me + 2 - 4 * pair
    cross = {"blk": across, "segment": 1 - seg}
    a = y * (1 - core) + z * core
    b = z * (1 - core) + y * core

    def at(da, dx, db, flip=0):
        spot = ((a + da) % SIDE) * (4 - 3 * core) + ((b + db) % SIDE) * (1 + 3 * core)
        return spot * 4 + ((pair + dx) % 2) * 2 + (core + flip) % 2

    loads = [
        pltpu.make_async_copy(src, dst, load_sem.at[i])
        for i, (src, dst) in enumerate([
            (channel_ref, channel_v), (orbitals_ref, orb_v), (target_ref, target_v),
            (coupling_ref, coupling_v), (slabs_ref, slab_v),
        ])
    ]
    for load in loads:
        load.start()

    near = [(0, 0), (1, 0), (3, 0), (0, 1), (2, 0), (1, 1), (3, 1), (2, 1)]
    partners = [at(da, dx, 0) for da, dx in near[1:]] + [at(da, dx, 0, 1) for da, dx in near]
    partners += [at(0, dx, db, 1) for db, dx in near if db] + [at(0, 0, db) for db in range(1, SIDE)]
    barrier = pltpu.get_barrier_semaphore()
    for partner in partners:
        pl.semaphore_signal(barrier, inc=1, device_id={"blk": partner})
    pl.semaphore_signal(barrier, inc=1, device_id=cross)

    def group(k, which, j, db):
        at_b = (b + db) % SIDE
        return c.at[which, 0, j, :, at_b] if k == 0 else c.at[which, 1, j, at_b]

    def chip(which, j, da, dx):
        pa = (a + da) % SIDE
        return c.at[which, core, j, pa * (1 - core) + b * core, b * (1 - core) + pa * core, (pair + dx) % 2]

    def each_core(do):
        for k in range(2):
            @pl.when(core == k)
            def _():
                do(k)

    def send(view, send_sem, recv_sem, device, dst=None):
        device = device if isinstance(device, dict) else {"blk": device}
        pltpu.make_async_remote_copy(
            src_ref=view, dst_ref=view if dst is None else dst,
            send_sem=send_sem, recv_sem=recv_sem, device_id=device,
        ).start()

    def arrived(sem, count):
        view = panel.at[0, pl.ds(0, count * rows), :]
        pltpu.make_async_copy(view, view, sem).wait()

    def make(j):
        picks = [
            channel_v[:, pl.ds(pl.multiple_of(seg * cols + (q * part + j * w), w), w)] for q in range(2)
        ]
        picks = jnp.concatenate(picks, axis=1)
        kinds = lax.broadcasted_iota(jnp.int32, (mine.shape[1], 2 * w), 0)
        onehot = jnp.where(kinds == picks, 1.0, 0.0).astype(jnp.bfloat16)
        got = jnp.dot(mine, onehot, preferred_element_type=jnp.float32).astype(jnp.bfloat16)
        for q in range(2):
            own[j, q] = got[:, q * w : (q + 1) * w]
        c[seg, core, j, y, z, pair, core] = own[j, core]

    def near_out(j):
        for i in NEAR:
            da, dx = near[i]
            recv = near_recv.at[j, i]
            if i:
                send(own.at[j, core], near_send.at[j], recv, at(da, dx, 0), c.at[seg, core, j, y, z, pair, core])
            send(
                own.at[j, 1 - core], near_send.at[j], recv, at(0, dx, da, 1),
                c.at[seg, 1 - core, j, y, z, pair, core],
            )

    def near_in(j):
        for i in NEAR:
            da, dx = near[i]
            arrived(near_recv.at[j, i], 2 if i else 1)
            view = chip(seg, j, -da, dx)
            for far in (2, 1, 3):
                send(view, far_send.at[j], far_recv.at[j, far - 1], at(0, 0, far))
            send(view, cross_send.at[j], cross_recv.at[j, 0], cross)
        each_core(lambda k: send(group(k, seg, j, 0), sib_send.at[j], sib_recv.at[j], sib))

    def far_in(j):
        for db in (1, 3, 2):
            arrived(far_recv.at[j, db - 1], 16)

            def do(k):
                view = group(k, seg, j, -db)
                send(view, sib_send.at[j], sib_recv.at[j], sib)
                if db not in RINGED[j]:
                    send(view, cross_send.at[j], cross_recv.at[j, db], cross)

            each_core(do)

    def other_in(j, db):
        arrived(other_recv.at[j, db - 1] if db in RINGED[j] else cross_recv.at[j, db], 16)

        def do(k):
            view = group(k, 1 - seg, j, -db)
            if db == 0:
                for far in RINGED[j]:
                    send(view, other_send.at[j], other_recv.at[j, far - 1], at(0, 0, far))
            send(view, over_send.at[j], over_recv.at[j, db], sib)

        each_core(do)

    def first(q, j):
        my_rows = pl.ds(pl.multiple_of(me * rows, rows), rows)

        def one(step, carry):
            at_y = (y + step) % SIDE
            count = slabs // SIDE
            left = slab_v[pl.ds(at_y * count, count)].reshape(count * rows, depth)
            got = jnp.dot(left, c[seg, q, j].reshape(depth, w), preferred_element_type=jnp.float32)
            half[q, j, pl.ds(at_y * count, count)] = got.astype(jnp.bfloat16).reshape(count, rows, w)

            def go(i, carry):
                slab = at_y * count + (me // 2 + i) % count
                peer = slab * 2 + q

                @pl.when(peer != me)
                def _():
                    send(half.at[q, j, slab], swap_send.at[j], swap_recv.at[j], peer, panel.at[j, my_rows, :])

                return carry

            return lax.fori_loop(0, count, go, carry)

        lax.fori_loop(0, SIDE, one, 0)

    def turn_group(q, j, db):
        top = pl.multiple_of((1 - seg) * cols + (q * part + j * w), w)
        if q == 0:
            at_z = (z - db) % SIDE
            for at_y in range(SIDE):
                start = pl.multiple_of((at_y * SIDE + at_z) * 4 * rows, 4 * rows)
                piece = c[1 - seg, 0, j, at_y, at_z].reshape(4 * rows, w)
                ct[pl.ds(top, w), pl.ds(start, 4 * rows)] = piece.T
        else:
            at_y = (y - db) % SIDE
            wide = SIDE * 4 * rows
            piece = c[1 - seg, 1, j, at_y].reshape(wide, w)
            ct[pl.ds(top, w), pl.ds(pl.multiple_of(at_y * wide, wide), wide)] = piece.T

    def others(items, before=()):
        waiting = list(before)
        for j, db in items:
            other_in(j, db)
            each_core(lambda k: turn_group(k, j, db))
            waiting.append((j, db))
            if len(waiting) > LAG:
                over_in(*waiting.pop(0))
        return waiting

    def over_in(j, db):
        arrived(over_recv.at[j, db], 16)
        each_core(lambda k: turn_group(1 - k, j, db))

    def turn(which):
        def one(i, carry):
            start = pl.multiple_of(i * 256, 256)
            for q in range(2):
                for j in range(PIECES):
                    top = pl.multiple_of(which * cols + (q * part + j * w), w)
                    piece = c[which, q, j, i // 2, pl.ds(i % 2 * 2, 2)].reshape(256, w)
                    ct[pl.ds(top, w), pl.ds(start, 256)] = piece.T
            return carry

        lax.fori_loop(0, depth // 256, one, 0)

    loads[0].wait()
    loads[1].wait()
    mine = orb_v[...]
    make(0)
    pl.semaphore_wait(barrier, len(partners) + 1)
    near_out(0)
    make(1)
    near_out(1)
    near_in(0)
    near_in(1)
    far_in(0)
    loads[4].wait()
    first(core, 0)
    for j in EARLY:
        other_in(j, 0)
    waiting = [(j, 0) for j in EARLY]
    arrived(sib_recv.at[0], blocks)
    first(1 - core, 0)
    far_in(1)
    first(core, 1)
    arrived(sib_recv.at[1], blocks)
    first(1 - core, 1)
    for j in range(PIECES):
        panel[j, pl.ds(pl.multiple_of(me * rows, rows), rows), :] = half[core, j, me // 2]
    turn(seg)

    loads[2].wait()
    loads[3].wait()
    nt = coupling_v.shape[0]
    kinds = lax.broadcasted_iota(jnp.int32, (nt, nch), 0)
    hot = jnp.where(kinds == target_v[...], 1.0, 0.0).astype(jnp.bfloat16)
    channel = lax.broadcasted_iota(jnp.int32, (share, nch), 1)
    line = lax.broadcasted_iota(jnp.int32, (share, nch), 0)
    pick = jnp.where(channel == line + me * share, 1.0, 0.0).astype(jnp.bfloat16)
    hot_rows = lax.dot_general(pick, hot, DIMS, preferred_element_type=jnp.float32).astype(jnp.bfloat16)
    table = coupling_v[...].astype(jnp.float32).astype(jnp.bfloat16)
    mixed = jnp.dot(hot_rows, table, preferred_element_type=jnp.float32).astype(jnp.bfloat16)
    angular = jnp.dot(mixed, hot, preferred_element_type=jnp.float32) * (1.0 / 16.0)
    angular_ref[...] = jnp.where(seg == 0, angular[:, :cols], angular[:, cols:])

    for j in EARLY:
        each_core(lambda k: turn_group(k, j, 0))
    waiting = others([(j, 0) for j in range(PIECES) if j not in EARLY] + list(FIRSTS), waiting)

    def out_at(j):
        return out_ref.at[me // 2, :, pl.ds(pl.multiple_of(core * part + j * w, w), w)]

    def second(j, which):
        def one(step, carry):
            at_y = 2 * which + (y + 1 + step) % 2
            count = nch // SIDE
            left = ct[pl.ds(pl.multiple_of(at_y * count, count), count), :]
            got = jnp.dot(left, panel[j], preferred_element_type=jnp.float32).astype(jnp.bfloat16)
            quarter[j, pl.ds(at_y * per_y, per_y)] = got.reshape(per_y, share, w)

            def go(i, carry):
                peer = at_y * per_y + (me + i) % per_y

                @pl.when(peer != me)
                def _():
                    send(quarter.at[j, peer], back_send.at[j], back_recv.at[j], peer, out_at(j))

                return carry

            return lax.fori_loop(0, per_y, go, carry)

        lax.fori_loop(0, SIDE // 2, one, 0)

    arrived(swap_recv.at[0], blocks - 1)
    second(0, seg)
    if LATE:
        pass
        arrived(swap_recv.at[1], blocks - 1)
        second(1, seg)
    for j, db in others(LASTS, waiting):
        over_in(j, db)
    second(0, 1 - seg)
    if not LATE:
        pass
        arrived(swap_recv.at[1], blocks - 1)
        second(1, seg)
    second(1, 1 - seg)
    kept = [pltpu.make_async_copy(quarter.at[j, me], out_at(j), own_sem.at[j]) for j in range(PIECES)]
    for copy in kept:
        copy.start()
    for copy in kept:
        copy.wait()

    for j in range(PIECES):
        last = quarter.at[j, pl.ds(0, blocks - 1)]
        arrived(near_send.at[j], 15)
        arrived(far_send.at[j], 48)
        arrived(sib_send.at[j], blocks)
        arrived(cross_send.at[j], 16 * (4 - len(RINGED[j])))
        if RINGED[j]:
            arrived(other_send.at[j], 16 * len(RINGED[j]))
        arrived(over_send.at[j], blocks)
        arrived(swap_send.at[j], blocks - 1)
        pltpu.make_async_copy(last, last, back_send.at[j]).wait()
        pltpu.make_async_copy(last, last, back_recv.at[j]).wait()


def on_device(slabs, orbitals, channel_orbital, channel_target, coupling):
    blocks = lax.axis_size("blk")
    count, rows, depth = slabs.shape
    nch = channel_orbital.shape[0]
    cols = nch // 2
    part = cols // 2
    w = part // PIECES
    share = nch // blocks
    hbm = pl.BlockSpec(memory_space=pltpu.HBM)
    dma = pltpu.SemaphoreType.DMA
    each = dma((PIECES,))
    vmem = pltpu.VMEM
    picked, angular = pl.pallas_call(
        body,
        out_shape=(
            jax.ShapeDtypeStruct((count, share, cols), jnp.bfloat16),
            jax.ShapeDtypeStruct((share, cols), jnp.float32),
        ),
        in_specs=[hbm] * 5,
        out_specs=(pl.BlockSpec(memory_space=pl.ANY), pl.BlockSpec(memory_space=vmem)),
        scratch_shapes=[
            vmem((count, rows, depth), jnp.bfloat16),
            vmem(orbitals.shape, jnp.bfloat16),
            vmem((1, nch), jnp.int32),
            vmem((1, nch), jnp.int32),
            vmem(coupling.shape, jnp.int32),
            vmem((PIECES, 2, rows, w), jnp.bfloat16),
            vmem((2, 2, PIECES, SIDE, SIDE, 2, 2, rows, w), jnp.bfloat16),
            vmem((nch, depth), jnp.bfloat16),
            vmem((2, PIECES, count, rows, w), jnp.bfloat16),
            vmem((PIECES, depth, w), jnp.bfloat16),
            vmem((PIECES, blocks, share, w), jnp.bfloat16),
            dma((5,)), each, dma((PIECES, 8)), each, dma((PIECES, 3)), each, each,
            each, dma((PIECES, 4)), each, dma((PIECES, 3)), each, dma((PIECES, 4)),
            each, each, each, each, each,
        ],
        compiler_params=pltpu.CompilerParams(
            collective_id=0, has_side_effects=True, vmem_limit_bytes=48 * 1024 * 1024
        ),
        name="transform",
    )(*[
        pltpu.with_memory_space_constraint(v, pltpu.HBM)
        for v in (slabs, orbitals, channel_orbital.reshape(1, nch), channel_target.reshape(1, nch), coupling)
    ])
    return (angular[None] * picked.astype(jnp.float32)).astype(jnp.bfloat16)


def solution(mesh):
    return jax.shard_map(
        on_device,
        mesh=mesh,
        in_specs=(P(None, "blk", None), P("blk", None), P(), P(), P()),
        out_specs=P(None, "blk", "segment"),
        check_vma=False,
    )
```

```python
import jax
import jax.numpy as jnp
from jax import lax
from jax.experimental import pallas as pl
from jax.experimental.pallas import tpu as pltpu
from jax.sharding import PartitionSpec as P

SIDE = 4
PIECES = 2
RINGED = ((), (1, 3))
EARLY = (1,)
FIRSTS = ((0, 1), (0, 3), (1, 1), (1, 3), (0, 2), (1, 2))
LASTS = ()
LATE = 0
LAG = 1
NEAR = (0, 3, 1, 2, 5, 6, 4, 7)
DIMS = (((1,), (1,)), ((), ()))


def body(
    slabs_ref, orbitals_ref, channel_ref, target_ref, coupling_ref,
    out_ref, angular_ref,
    slab_v, orb_v, channel_v, target_v, coupling_v, own, c, ct, half, panel, quarter,
    load_sem, near_send, near_recv, far_send, far_recv, sib_send, sib_recv,
    cross_send, cross_recv, other_send, other_recv, over_send, over_recv,
    swap_send, swap_recv, back_send, back_recv, own_sem,
):
    slabs, rows, depth = slab_v.shape
    blocks = depth // rows
    nch = ct.shape[0]
    cols = nch // 2
    part = cols // 2
    w = part // PIECES
    share = nch // blocks
    per_y = blocks // SIDE

    seg = lax.axis_index("segment")
    me = lax.axis_index("blk")
    core = me % 2
    pair = (me // 2) % 2
    z = (me // 4) % SIDE
    y = me // (4 * SIDE)
    sib = me + 1 - 2 * core
    across = me + 2 - 4 * pair
    cross = {"blk": across, "segment": 1 - seg}
    a = y * (1 - core) + z * core
    b = z * (1 - core) + y * core

    def at(da, dx, db, flip=0):
        spot = ((a + da) % SIDE) * (4 - 3 * core) + ((b + db) % SIDE) * (1 + 3 * core)
        return spot * 4 + ((pair + dx) % 2) * 2 + (core + flip) % 2

    loads = [
        pltpu.make_async_copy(src, dst, load_sem.at[i])
        for i, (src, dst) in enumerate([
            (channel_ref, channel_v), (orbitals_ref, orb_v), (target_ref, target_v),
            (coupling_ref, coupling_v), (slabs_ref, slab_v),
        ])
    ]
    for load in loads:
        load.start()

    near = [(0, 0), (1, 0), (3, 0), (0, 1), (2, 0), (1, 1), (3, 1), (2, 1)]
    partners = [at(da, dx, 0) for da, dx in near[1:]] + [at(da, dx, 0, 1) for da, dx in near]
    partners += [at(0, dx, db, 1) for db, dx in near if db] + [at(0, 0, db) for db in range(1, SIDE)]
    barrier = pltpu.get_barrier_semaphore()
    for partner in partners:
        pl.semaphore_signal(barrier, inc=1, device_id={"blk": partner})
    pl.semaphore_signal(barrier, inc=1, device_id=cross)

    def group(k, which, j, db):
        at_b = (b + db) % SIDE
        return c.at[which, 0, j, :, at_b] if k == 0 else c.at[which, 1, j, at_b]

    def chip(which, j, da, dx):
        pa = (a + da) % SIDE
        return c.at[which, core, j, pa * (1 - core) + b * core, b * (1 - core) + pa * core, (pair + dx) % 2]

    def each_core(do):
        for k in range(2):
            @pl.when(core == k)
            def _():
                do(k)

    def send(view, send_sem, recv_sem, device, dst=None):
        device = device if isinstance(device, dict) else {"blk": device}
        pltpu.make_async_remote_copy(
            src_ref=view, dst_ref=view if dst is None else dst,
            send_sem=send_sem, recv_sem=recv_sem, device_id=device,
        ).start()

    def arrived(sem, count):
        view = panel.at[0, pl.ds(0, count * rows), :]
        pltpu.make_async_copy(view, view, sem).wait()

    def make(j):
        picks = [
            channel_v[:, pl.ds(pl.multiple_of(seg * cols + (q * part + j * w), w), w)] for q in range(2)
        ]
        picks = jnp.concatenate(picks, axis=1)
        kinds = lax.broadcasted_iota(jnp.int32, (mine.shape[1], 2 * w), 0)
        onehot = jnp.where(kinds == picks, 1.0, 0.0).astype(jnp.bfloat16)
        got = jnp.dot(mine, onehot, preferred_element_type=jnp.float32).astype(jnp.bfloat16)
        for q in range(2):
            own[j, q] = got[:, q * w : (q + 1) * w]
        c[seg, core, j, y, z, pair, core] = own[j, core]

    def near_out(j):
        for i in NEAR:
            da, dx = near[i]
            recv = near_recv.at[j, i]
            if i:
                send(own.at[j, core], near_send.at[j], recv, at(da, dx, 0), c.at[seg, core, j, y, z, pair, core])
            send(
                own.at[j, 1 - core], near_send.at[j], recv, at(0, dx, da, 1),
                c.at[seg, 1 - core, j, y, z, pair, core],
            )

    def near_in(j):
        for i in NEAR:
            da, dx = near[i]
            arrived(near_recv.at[j, i], 2 if i else 1)
            view = chip(seg, j, -da, dx)
            for far in (2, 1, 3):
                send(view, far_send.at[j], far_recv.at[j, far - 1], at(0, 0, far))
            send(view, cross_send.at[j], cross_recv.at[j, 0], cross)
        each_core(lambda k: send(group(k, seg, j, 0), sib_send.at[j], sib_recv.at[j], sib))

    def far_in(j):
        for db in (1, 3, 2):
            arrived(far_recv.at[j, db - 1], 16)

            def do(k):
                view = group(k, seg, j, -db)
                if db not in RINGED[j]:
                    send(view, cross_send.at[j], cross_recv.at[j, db], cross)
                send(view, sib_send.at[j], sib_recv.at[j], sib)

            each_core(do)

    def other_in(j, db):
        arrived(other_recv.at[j, db - 1] if db in RINGED[j] else cross_recv.at[j, db], 16)

        def do(k):
            view = group(k, 1 - seg, j, -db)
            if db == 0:
                for far in RINGED[j]:
                    send(view, other_send.at[j], other_recv.at[j, far - 1], at(0, 0, far))
            send(view, over_send.at[j], over_recv.at[j, db], sib)

        each_core(do)

    def first(q, j):
        my_rows = pl.ds(pl.multiple_of(me * rows, rows), rows)

        def one(step, carry):
            at_y = (y + step) % SIDE
            count = slabs // SIDE
            left = slab_v[pl.ds(at_y * count, count)].reshape(count * rows, depth)
            got = jnp.dot(left, c[seg, q, j].reshape(depth, w), preferred_element_type=jnp.float32)
            half[q, j, pl.ds(at_y * count, count)] = got.astype(jnp.bfloat16).reshape(count, rows, w)

            def go(i, carry):
                slab = at_y * count + (me // 2 + 3 * i) % count
                peer = slab * 2 + q

                @pl.when(peer != me)
                def _():
                    send(half.at[q, j, slab], swap_send.at[j], swap_recv.at[j], peer, panel.at[j, my_rows, :])

                return carry

            return lax.fori_loop(0, count, go, carry)

        lax.fori_loop(0, SIDE, one, 0)

    def turn_group(q, j, db):
        top = pl.multiple_of((1 - seg) * cols + (q * part + j * w), w)
        if q == 0:
            at_z = (z - db) % SIDE
            for at_y in range(SIDE):
                start = pl.multiple_of((at_y * SIDE + at_z) * 4 * rows, 4 * rows)
                piece = c[1 - seg, 0, j, at_y, at_z].reshape(4 * rows, w)
                ct[pl.ds(top, w), pl.ds(start, 4 * rows)] = piece.T
        else:
            at_y = (y - db) % SIDE
            wide = SIDE * 4 * rows
            piece = c[1 - seg, 1, j, at_y].reshape(wide, w)
            ct[pl.ds(top, w), pl.ds(pl.multiple_of(at_y * wide, wide), wide)] = piece.T

    def others(items, before=()):
        waiting = list(before)
        for j, db in items:
            other_in(j, db)
            each_core(lambda k: turn_group(k, j, db))
            waiting.append((j, db))
            if len(waiting) > LAG:
                over_in(*waiting.pop(0))
        return waiting

    def over_in(j, db):
        arrived(over_recv.at[j, db], 16)
        each_core(lambda k: turn_group(1 - k, j, db))

    def turn(which):
        def one(i, carry):
            start = pl.multiple_of(i * 256, 256)
            for q in range(2):
                for j in range(PIECES):
                    top = pl.multiple_of(which * cols + (q * part + j * w), w)
                    piece = c[which, q, j, i // 2, pl.ds(i % 2 * 2, 2)].reshape(256, w)
                    ct[pl.ds(top, w), pl.ds(start, 256)] = piece.T
            return carry

        lax.fori_loop(0, depth // 256, one, 0)

    loads[0].wait()
    loads[1].wait()
    mine = orb_v[...]
    make(0)
    pl.semaphore_wait(barrier, len(partners) + 1)
    near_out(0)
    make(1)
    near_out(1)
    near_in(0)
    near_in(1)
    far_in(0)
    loads[4].wait()
    first(core, 0)
    for j in EARLY:
        other_in(j, 0)
    waiting = [(j, 0) for j in EARLY]
    arrived(sib_recv.at[0], blocks)
    first(1 - core, 0)
    far_in(1)
    first(core, 1)
    arrived(sib_recv.at[1], blocks)
    first(1 - core, 1)
    for j in range(PIECES):
        panel[j, pl.ds(pl.multiple_of(me * rows, rows), rows), :] = half[core, j, me // 2]
    turn(seg)

    loads[2].wait()
    loads[3].wait()
    nt = coupling_v.shape[0]
    kinds = lax.broadcasted_iota(jnp.int32, (nt, nch), 0)
    hot = jnp.where(kinds == target_v[...], 1.0, 0.0).astype(jnp.bfloat16)
    channel = lax.broadcasted_iota(jnp.int32, (share, nch), 1)
    line = lax.broadcasted_iota(jnp.int32, (share, nch), 0)
    pick = jnp.where(channel == line + me * share, 1.0, 0.0).astype(jnp.bfloat16)
    hot_rows = lax.dot_general(pick, hot, DIMS, preferred_element_type=jnp.float32).astype(jnp.bfloat16)
    table = coupling_v[...].astype(jnp.float32).astype(jnp.bfloat16)
    mixed = jnp.dot(hot_rows, table, preferred_element_type=jnp.float32).astype(jnp.bfloat16)
    angular = jnp.dot(mixed, hot, preferred_element_type=jnp.float32) * (1.0 / 16.0)
    angular_ref[...] = jnp.where(seg == 0, angular[:, :cols], angular[:, cols:])

    for j in EARLY:
        each_core(lambda k: turn_group(k, j, 0))
    waiting = others([(j, 0) for j in range(PIECES) if j not in EARLY] + list(FIRSTS), waiting)

    def out_at(j):
        return out_ref.at[me // 2, :, pl.ds(pl.multiple_of(core * part + j * w, w), w)]

    def second(j, which):
        def one(step, carry):
            at_y = 2 * which + (y + 1 + step) % 2
            count = nch // SIDE
            left = ct[pl.ds(pl.multiple_of(at_y * count, count), count), :]
            got = jnp.dot(left, panel[j], preferred_element_type=jnp.float32).astype(jnp.bfloat16)
            quarter[j, pl.ds(at_y * per_y, per_y)] = got.reshape(per_y, share, w)

            def go(i, carry):
                peer = at_y * per_y + (me + 5 * i) % per_y

                @pl.when(peer != me)
                def _():
                    send(quarter.at[j, peer], back_send.at[j], back_recv.at[j], peer, out_at(j))

                return carry

            return lax.fori_loop(0, per_y, go, carry)

        lax.fori_loop(0, SIDE // 2, one, 0)

    arrived(swap_recv.at[0], blocks - 1)
    second(0, seg)
    if LATE:
        pass
        arrived(swap_recv.at[1], blocks - 1)
        second(1, seg)
    for j, db in others(LASTS, waiting):
        over_in(j, db)
    second(0, 1 - seg)
    if not LATE:
        pass
        arrived(swap_recv.at[1], blocks - 1)
        second(1, seg)
    second(1, 1 - seg)
    kept = [pltpu.make_async_copy(quarter.at[j, me], out_at(j), own_sem.at[j]) for j in range(PIECES)]
    for copy in kept:
        copy.start()
    for copy in kept:
        copy.wait()

    for j in range(PIECES):
        last = quarter.at[j, pl.ds(0, blocks - 1)]
        arrived(near_send.at[j], 15)
        arrived(far_send.at[j], 48)
        arrived(sib_send.at[j], blocks)
        arrived(cross_send.at[j], 16 * (4 - len(RINGED[j])))
        if RINGED[j]:
            arrived(other_send.at[j], 16 * len(RINGED[j]))
        arrived(over_send.at[j], blocks)
        arrived(swap_send.at[j], blocks - 1)
        pltpu.make_async_copy(last, last, back_send.at[j]).wait()
        pltpu.make_async_copy(last, last, back_recv.at[j]).wait()


def on_device(slabs, orbitals, channel_orbital, channel_target, coupling):
    blocks = lax.axis_size("blk")
    count, rows, depth = slabs.shape
    nch = channel_orbital.shape[0]
    cols = nch // 2
    part = cols // 2
    w = part // PIECES
    share = nch // blocks
    hbm = pl.BlockSpec(memory_space=pltpu.HBM)
    dma = pltpu.SemaphoreType.DMA
    each = dma((PIECES,))
    vmem = pltpu.VMEM
    picked, angular = pl.pallas_call(
        body,
        out_shape=(
            jax.ShapeDtypeStruct((count, share, cols), jnp.bfloat16),
            jax.ShapeDtypeStruct((share, cols), jnp.float32),
        ),
        in_specs=[hbm] * 5,
        out_specs=(pl.BlockSpec(memory_space=pl.ANY), pl.BlockSpec(memory_space=vmem)),
        scratch_shapes=[
            vmem((count, rows, depth), jnp.bfloat16),
            vmem(orbitals.shape, jnp.bfloat16),
            vmem((1, nch), jnp.int32),
            vmem((1, nch), jnp.int32),
            vmem(coupling.shape, jnp.int32),
            vmem((PIECES, 2, rows, w), jnp.bfloat16),
            vmem((2, 2, PIECES, SIDE, SIDE, 2, 2, rows, w), jnp.bfloat16),
            vmem((nch, depth), jnp.bfloat16),
            vmem((2, PIECES, count, rows, w), jnp.bfloat16),
            vmem((PIECES, depth, w), jnp.bfloat16),
            vmem((PIECES, blocks, share, w), jnp.bfloat16),
            dma((5,)), each, dma((PIECES, 8)), each, dma((PIECES, 3)), each, each,
            each, dma((PIECES, 4)), each, dma((PIECES, 3)), each, dma((PIECES, 4)),
            each, each, each, each, each,
        ],
        compiler_params=pltpu.CompilerParams(
            collective_id=0, has_side_effects=True, vmem_limit_bytes=48 * 1024 * 1024
        ),
        name="transform",
    )(*[
        pltpu.with_memory_space_constraint(v, pltpu.HBM)
        for v in (slabs, orbitals, channel_orbital.reshape(1, nch), channel_target.reshape(1, nch), coupling)
    ])
    return (angular[None] * picked.astype(jnp.float32)).astype(jnp.bfloat16)


def solution(mesh):
    return jax.shard_map(
        on_device,
        mesh=mesh,
        in_specs=(P(None, "blk", None), P("blk", None), P(), P(), P()),
        out_specs=P(None, "blk", "segment"),
        check_vma=False,
    )
```
